32 devices in a mesh: parts: 2 (over x), wide: 16 (over z, y, core).
Axes of the slice: x: 2, y: 2, z: 4, core: 2. Of those that a mesh axis runs over, the one named last changes fastest.
Arguments:
- voxels: bfloat16 [32768, 256], P(('parts', 'wide')), parts along dimension 0, may hold values from -16 to 16
- regular_window: int32 [32768], P(('parts', 'wide')), parts along dimension 0, may hold values from 0 to 127, never falling along the last dimension, each value on 1 to 256 neighbouring positions
- shifted_window: int32 [32768], P(('parts', 'wide')), parts along dimension 0, may hold values from 0 to 127, never falling along the last dimension, each value on 1 to 256 neighbouring positions
- dest: int32 [32768], P(('parts', 'wide')), parts along dimension 0, may hold values from 0 to 16383, as said below
- w_qkv: bfloat16 [2, 256, 768], replicated, may hold values from -0.375 to 0.375
- w_out: bfloat16 [2, 256, 256], replicated, may hold values from -1.5 to 1.5
- gain: float32 [2, 256], replicated, may hold values from 0.1 to 1.9
- temper: float32 [2, 8], replicated, may hold values from 0.5 to 6
Outputs:
- shifted_out: bfloat16 [32768, 256], P(('parts', 'wide')), parts along dimension 0
The draws below stay inside these ranges and needn't reach their ends.
There are 2 independent parts, one for each index of `parts`. The reference program is written for one: setup_inputs(seed, part) draws one part's arguments, and reference() takes and returns one part's arrays. A program takes and returns all parts, laid end to end along the dimension named above; an argument that names none is the same for every part. Nothing has to cross between parts.
Inputs may be any that keep to these rules, and one draw needn't show every extreme that they name: `regular_window`: window ids never fall along the order; every window has 1 to 256 voxels and one has exactly 256. `shifted_window`: window ids never fall along the order; every window has 1 to 256 voxels and one has exactly 256. dest is a permutation. Counting blocks of 1024 consecutive positions, at most 128 voxels go from one block of the regular order to one block of the shifted order, and some pair reaches 128; the count from a block to the block k places further along, cyclically, is the same for every block.
All inputs are finite; a program needn't handle non-finite values.
Results may differ from the reference program's by a relative error of at most 0.007.
The reference program's roundings to bfloat16 on the way (of `projected`, `weights`, `attended`, `sublayer`, `first` and `moved`) count: a program that leaves them out, or rounds other values in their place, can miss the bound.
Values may be sent and summed in bfloat16 or wider, within the bound.
A program may use at most 64 MiB of HBM per device.

```python
import math
import jax
import jax.numpy as jnp
import numpy as np
from jax import lax

C = 256
HEADS = 8
VOX_DEV = 1024
WIN = 256
VOXELS = 16384
WINDOWS = 128


def draw_voxels(key, part):
    first_key = jax.random.fold_in(key, 0)
    base = jax.random.normal(first_key, (VOXELS, C), jnp.float32)
    values = jnp.clip(base, -6.0, 6.0)
    return values.astype(jnp.bfloat16)


def draw_temper(key, part):
    uniforms = jax.random.uniform(key, (2, HEADS), jnp.float32)
    values = jnp.exp(math.log(0.5) + uniforms * math.log(8.0))
    return values.astype(jnp.float32)


def draw_dest(key, part):
    groups = VOXELS // VOX_DEV
    share = VOX_DEV // groups
    first_key, second_key, third_key, fourth_key = jax.random.split(key, 4)
    lifts = jax.random.randint(first_key, (groups // 2,), 0, share + 1).astype(jnp.int32)
    lifts = lifts.at[0].set(share)
    amounts = jnp.stack([share + lifts, share - lifts], axis=1).reshape(groups)
    amounts = amounts[jax.random.permutation(second_key, groups)]
    bounds = jnp.cumsum(amounts).astype(jnp.int32)
    local_order = jax.vmap(lambda one_key: jax.random.permutation(one_key, VOX_DEV))(jax.random.split(third_key, groups))
    local_order = local_order.astype(jnp.int32)
    offsets = jnp.sum((bounds[None, None, :] <= local_order[:, :, None]).astype(jnp.int32), axis=2)
    target = (jnp.arange(groups, dtype=jnp.int32)[:, None] + offsets) % groups
    arrival = jax.vmap(lambda one_key: jax.random.permutation(one_key, VOX_DEV))(jax.random.split(fourth_key, groups))
    arrival = arrival.astype(jnp.int32)
    final_slot = arrival[target, local_order]
    return (target * VOX_DEV + final_slot).reshape(VOXELS).astype(jnp.int32)


def profile(count, total, reach, slope):
    weights = [(1 << 20) // math.isqrt(standing ** slope) + 1 for standing in range(2, count + 1)]
    spare, counts = total - reach - (count - 1), [1] * (count - 1)
    while spare > 0:
        movable = [i for i in range(count - 1) if counts[i] < reach]
        whole, budget = sum([weights[i] for i in movable]), spare
        for i in movable:
            extra = min(reach - counts[i], max(1, budget * weights[i] // whole), spare)
            counts[i] = counts[i] + extra
            spare = spare - extra
    return np.array([reach] + counts)


def uneven_parts(own_key, number_of, total, bound, lean):
    if number_of == 2:
        one = jax.random.randint(own_key, (), max(1, total - bound), min(bound, total - 1) + 1)
        return jnp.stack([one, total - one])
    tallies = jnp.asarray(profile(number_of, total, bound, lean), jnp.int32)
    pairs = (number_of - 1) // 2
    source_of, sink = tallies[1:1 + 2 * pairs:2], tallies[2:2 + 2 * pairs:2]
    room = jnp.minimum(source_of - 1, bound - sink)
    shifted = jax.random.randint(jax.random.fold_in(own_key, 1), (pairs,), 0, 1 << 20) % (room + 1)
    tallies = tallies.at[1:1 + 2 * pairs:2].set(source_of - shifted).at[2:2 + 2 * pairs:2].set(sink + shifted)
    return tallies[jax.random.permutation(jax.random.fold_in(own_key, 2), number_of)]


def centred(key, dims, width, bound, kind=jnp.bfloat16):
    return jnp.clip(width * jax.random.normal(key, dims, jnp.float32), -bound, bound).astype(kind)


def setup_inputs(seed: int = 0, part: int = 0) -> dict:
    keys = jax.random.split(jax.random.key(seed), 9)
    part_keys = jax.random.split(jax.random.fold_in(keys[8], part), 9)
    voxels = draw_voxels(jax.random.fold_in(jax.random.fold_in(keys[8], part), 71), part)
    regular_window = jnp.searchsorted(jnp.cumsum(uneven_parts(part_keys[1], WINDOWS, VOXELS, WIN, 1)), jnp.arange(VOXELS), side="right").astype(jnp.int32)
    shifted_window = jnp.searchsorted(jnp.cumsum(uneven_parts(part_keys[2], WINDOWS, VOXELS, WIN, 1)), jnp.arange(VOXELS), side="right").astype(jnp.int32)
    dest = draw_dest(jax.random.fold_in(jax.random.fold_in(keys[8], part), 71), part)
    w_qkv = centred(keys[4], (2, C, 3 * C), C ** -0.5, 0.375)
    w_out = centred(keys[5], (2, C, C), (C // 16) ** -0.5, 1.5)
    gain = jnp.clip(1.0 + 0.18 * jax.random.normal(keys[6], (2, C), jnp.float32), 0.1, 1.9)
    temper = draw_temper(jax.random.fold_in(keys[8], 71), part)
    return {"voxels": voxels, "regular_window": regular_window, "shifted_window": shifted_window, "dest": dest, "w_qkv": w_qkv, "w_out": w_out, "gain": gain, "temper": temper}


epsilon = 1e-05
masked_score = -1e+30

def settle(hidden, attended, w_out_layer, gain_layer):
    summed = hidden.astype(jnp.float32) + jnp.dot(attended, w_out_layer, preferred_element_type=jnp.float32)
    center = lax.optimization_barrier(jnp.mean(summed, axis=1, keepdims=True))
    spread = lax.optimization_barrier(jnp.mean(jnp.square(summed - center), axis=1, keepdims=True))
    return ((summed - center) * lax.rsqrt(spread + epsilon) * gain_layer).astype(jnp.bfloat16)

def sublayer(hidden, window_ids, w_qkv_layer, w_out_layer, gain_layer, temper_layer):
    total_rows = hidden.shape[0]
    channels = hidden.shape[1]
    head_dim = channels // HEADS
    projected = jnp.dot(hidden, w_qkv_layer, preferred_element_type=jnp.float32).astype(jnp.bfloat16)
    queries = projected[:, :channels]
    padded = jnp.pad(projected[:, channels:], ((WIN, WIN), (0, 0)))
    marks = (window_ids + 1).astype(jnp.int32)
    marks_pad = jnp.pad(marks, (WIN, WIN))
    factor = temper_layer * (1.0 / math.sqrt(head_dim))
    block_rows = math.gcd(total_rows, 512)
    key_rows = block_rows + 2 * WIN

    def one_block(number):
        first_row = (number * block_rows).astype(jnp.int32)
        query_block = lax.dynamic_slice_in_dim(queries, first_row, block_rows, 0).astype(jnp.float32)
        query_block = query_block.reshape(block_rows, HEADS, head_dim)
        key_block = lax.dynamic_slice_in_dim(padded, first_row, key_rows, 0).astype(jnp.float32)
        keys_part = key_block[:, :channels].reshape(key_rows, HEADS, head_dim)
        values_part = key_block[:, channels:].reshape(key_rows, HEADS, head_dim)
        mark_query = lax.dynamic_slice_in_dim(marks, first_row, block_rows, 0)
        mark_key = lax.dynamic_slice_in_dim(marks_pad, first_row, key_rows, 0)
        same_window = (mark_query[:, None] == mark_key[None, :])[None]
        scores = jnp.einsum('qhd,khd->hqk', query_block, keys_part) * factor[:, None, None]
        scores = jnp.where(same_window, scores, masked_score)
        highest = lax.optimization_barrier(jnp.max(scores, axis=2, keepdims=True))
        exponents = jnp.where(same_window, jnp.exp(scores - highest), 0.0)
        totals = lax.optimization_barrier(jnp.sum(exponents, axis=2, keepdims=True))
        weights = (exponents / totals).astype(jnp.bfloat16)
        result = jnp.einsum('hqk,khd->qhd', weights.astype(jnp.float32), values_part)
        return result.reshape(block_rows, channels).astype(jnp.bfloat16)
    attended = lax.map(one_block, jnp.arange(total_rows // block_rows, dtype=jnp.int32))
    attended = attended.reshape(total_rows, channels)
    return settle(hidden, attended, w_out_layer, gain_layer)

def reference(voxels, regular_window, shifted_window, dest, w_qkv, w_out, gain, temper):
    first = sublayer(voxels, regular_window, w_qkv[0], w_out[0], gain[0], temper[0])
    moved = jnp.zeros_like(first).at[dest.astype(jnp.int32)].set(first)
    return sublayer(moved, shifted_window, w_qkv[1], w_out[1], gain[1], temper[1])
```

```python
import functools
import math

import jax
import jax.numpy as jnp
from jax import lax
from jax.experimental import pallas as pl
from jax.experimental.pallas import tpu as pltpu
from jax.sharding import PartitionSpec as P

HEADS = 8
LANES = 128

epsilon = 1e-05
apart = 2.0**100

BF = jnp.bfloat16
F32 = jnp.float32
NT = (((1,), (1,)), ((), ()))


def codes(marks_row, sign_of_equal):
    count = marks_row.shape[1]
    place = lax.broadcasted_iota(jnp.int32, (LANES, count), 0)
    bit = (jnp.broadcast_to(marks_row, (LANES, count)) >> (place & 31)) & 1
    flag = jnp.where(place < LANES // 2, bit, 1 - bit).astype(F32)
    if sign_of_equal:
        return jnp.transpose(flag).astype(BF)
    return jnp.transpose((flag - 1.0) * apart).astype(BF)


def project_keys(h, marks_row, w_ref, k_ref, v_ref, first_row):
    rows, channels = h.shape
    half = channels // 2
    kv = jnp.dot(h, w_ref[:, channels:], preferred_element_type=F32).astype(BF)
    code = codes(marks_row, False)
    for g in range(2):
        at = pl.ds(first_row, rows)
        k_ref[g, at, :half] = kv[:, g * half : (g + 1) * half]
        k_ref[g, at, half:] = code
        v_ref[g, at, :] = kv[:, channels + g * half : channels + (g + 1) * half]


def attend(h, marks_row, w_ref, wo_ref, gain_row, factors, k_ref, v_ref, first_key, key_rows):
    rows, channels = h.shape
    half = channels // 2
    head_dim = channels // HEADS
    per_half = HEADS // 2
    q = jnp.dot(h, w_ref[:, :channels], preferred_element_type=F32).astype(BF)
    code = codes(marks_row, True)
    head_of_lane = lax.broadcasted_iota(jnp.int32, (rows, half), 1) // head_dim
    halves = []
    for g in range(2):
        q_half = q[:, g * half : (g + 1) * half]
        keys = k_ref[g, pl.ds(first_key, key_rows), :]
        values = v_ref[g, pl.ds(first_key, key_rows), :]
        out = jnp.zeros((rows, half), F32)
        for j in range(per_half):
            mine = head_of_lane == j
            query = jnp.concatenate([jnp.where(mine, q_half, jnp.zeros_like(q_half)), code], axis=1)
            s = lax.dot_general(query, keys, NT, preferred_element_type=F32)
            top = jnp.max(s, axis=1, keepdims=True)
            e = jnp.exp2((s - top) * factors[g * per_half + j])
            p = (e * (1.0 / jnp.sum(e, axis=1, keepdims=True))).astype(BF)
            out = jnp.where(mine, jnp.dot(p, values, preferred_element_type=F32), out)
        halves.append(out.astype(BF))
    attended = jnp.concatenate(halves, axis=1)
    summed = h.astype(F32) + jnp.dot(attended, wo_ref[...], preferred_element_type=F32)
    center = jnp.mean(summed, axis=1, keepdims=True)
    shifted = summed - center
    spread = jnp.mean(jnp.square(shifted), axis=1, keepdims=True)
    return (shifted * lax.rsqrt(spread + epsilon) * gain_row).astype(BF)


def sublayer_kernel(rim, block, fac_ref, h_ref, m_ref, w_ref, wo_ref, gain_ref, out_ref, k_ref, v_ref):
    total = out_ref.shape[0]
    for r in range(0, total + 2 * rim, rim):
        project_keys(h_ref[r : r + rim, :], m_ref[:, r : r + rim], w_ref, k_ref, v_ref, r)
    factors = [fac_ref[j] for j in range(HEADS)]
    for r in range(0, total, block):
        out_ref[r : r + block, :] = attend(
            h_ref[rim + r : rim + r + block, :],
            m_ref[:, rim + r : rim + r + block],
            w_ref, wo_ref, gain_ref[...], factors, k_ref, v_ref, r, block + 2 * rim,
        )


def extended(block, axis, width):
    count = lax.axis_size(axis)
    forward = [(i, i + 1) for i in range(count - 1)]
    backward = [(target, source) for source, target in forward]
    low = lax.ppermute(block[-width:], axis, forward)
    high = lax.ppermute(block[:width], axis, backward)
    return jnp.concatenate([low, block, high], axis=0)


def sublayer(hidden, window_ids, w_qkv_layer, w_out_layer, gain_layer, temper_layer):
    rows, channels = hidden.shape
    rim = rows // 4
    factor = temper_layer * (1.0 / math.sqrt(channels // HEADS)) * math.log2(math.e)
    padded = extended(hidden, "wide", rim)
    marks = extended(window_ids + 1, "wide", rim)[None, :]
    vmem = pl.BlockSpec(memory_space=pltpu.VMEM)
    return pl.pallas_call(
        functools.partial(sublayer_kernel, rim, rim),
        out_shape=jax.ShapeDtypeStruct((rows, channels), BF),
        in_specs=[pl.BlockSpec(memory_space=pltpu.SMEM)] + [vmem] * 5,
        out_specs=vmem,
        scratch_shapes=[pltpu.VMEM((2, rows + 2 * rim, channels), BF), pltpu.VMEM((2, rows + 2 * rim, channels // 2), BF)],
        compiler_params=pltpu.CompilerParams(vmem_limit_bytes=48 << 20),
    )(factor, padded, marks, w_qkv_layer, w_out_layer, gain_layer[None, :])


def regroup_rows(first, dest):
    local_rows = first.shape[0]
    channels = first.shape[1]
    devices = lax.axis_size("wide")
    capacity = 2 * local_rows // devices
    target = dest // local_rows
    slot_within = dest - target * local_rows
    matches = (target[:, None] == jnp.arange(devices, dtype=jnp.int32)[None, :]).astype(jnp.int32)
    position = jnp.sum(jnp.cumsum(matches, axis=0) * matches, axis=1) - 1
    buffer_row = target * capacity + position
    outgoing = jnp.zeros((devices * capacity, channels), jnp.bfloat16).at[buffer_row].set(first)
    slot_list = (
        jnp.full((devices * capacity,), local_rows, jnp.int32).at[buffer_row].set(slot_within)
    )
    arrived, arrived_slots = (
        lax.all_to_all(outgoing, "wide", split_axis=0, concat_axis=0, tiled=True),
        lax.all_to_all(slot_list, "wide", split_axis=0, concat_axis=0, tiled=True),
    )
    return (
        jnp.zeros((local_rows, channels), jnp.bfloat16).at[arrived_slots].set(arrived, mode="drop")
    )


def body(voxels, regular_window, shifted_window, dest, w_qkv, w_out, gain, temper):
    first = sublayer(voxels, regular_window, w_qkv[0], w_out[0], gain[0], temper[0])
    moved = regroup_rows(first, dest)
    return sublayer(moved, shifted_window, w_qkv[1], w_out[1], gain[1], temper[1])


def solution(mesh):
    spread = P(("parts", "wide"))
    wide_rows = P(("parts", "wide"), None)
    return jax.shard_map(
        body,
        mesh=mesh,
        in_specs=(wide_rows, spread, spread, spread, P(), P(), P(), P()),
        out_specs=wide_rows,
        check_vma=False,
    )
```

```python
import functools
import math

import jax
import jax.numpy as jnp
from jax import lax
from jax.experimental import pallas as pl
from jax.experimental.pallas import tpu as pltpu
from jax.sharding import PartitionSpec as P

HEADS = 8
LANES = 128
GROUPS = 2

epsilon = 1e-05
apart = 2.0**100

BF = jnp.bfloat16
F32 = jnp.float32
NT = (((1,), (1,)), ((), ()))


def bit_flags(marks_row):
    count = marks_row.shape[1]
    place = lax.broadcasted_iota(jnp.int32, (LANES, count), 0)
    bit = (jnp.broadcast_to(marks_row, (LANES, count)) >> (place & 31)) & 1
    return jnp.where(place < LANES // 2, bit, 1 - bit).astype(F32)


def project_keys(h, marks_row, w, k_ref, v_ref, first):
    rows, channels = h.shape
    half = channels // GROUPS
    kv = jnp.dot(h, w[:, channels:], preferred_element_type=F32)
    code = ((bit_flags(marks_row) - 1.0) * apart).astype(BF)
    at = pl.ds(first, rows)
    for g in range(GROUPS):
        k_ref[g, :half, at] = jnp.transpose(kv[:, g * half : (g + 1) * half]).astype(BF)
        k_ref[g, half:, at] = code
        v_ref[g, at, :] = kv[:, channels + g * half : channels + (g + 1) * half].astype(BF)


def attend(h, marks_row, layer, fac_ref, w, w_out, gain_row, k_ref, v_ref, q_ref, a_ref, first_key, key_rows):
    rows, channels = h.shape
    half = channels // GROUPS
    head_dim = channels // HEADS
    each = HEADS // GROUPS
    q = jnp.dot(h, w[:, :channels], preferred_element_type=F32).astype(BF)
    code = jnp.transpose(bit_flags(marks_row)).astype(BF)
    head_of_lane = lax.broadcasted_iota(jnp.int32, (rows, half), 1) // head_dim
    for g in range(GROUPS):
        q_ref[g] = q[:, g * half : (g + 1) * half]

    def group(g, carry):
        q_half = q_ref[g]
        keys = k_ref[g, :, pl.ds(first_key, key_rows)]
        values = v_ref[g, pl.ds(first_key, key_rows), :]
        out = jnp.zeros((rows, half), F32)
        for j in range(each):
            mine = head_of_lane == j
            query = jnp.concatenate([jnp.where(mine, q_half, jnp.zeros_like(q_half)), code], axis=1)
            s = jnp.dot(query, keys, preferred_element_type=F32)
            top = jnp.max(s, axis=1, keepdims=True)
            e = jnp.exp2((s - top) * fac_ref[layer, g * each + j])
            p = (e * (1.0 / jnp.sum(e, axis=1, keepdims=True))).astype(BF)
            out = jnp.where(mine, jnp.dot(p, values, preferred_element_type=F32), out)
        a_ref[g] = out.astype(BF)
        return carry

    lax.fori_loop(0, GROUPS, group, 0)
    attended = jnp.concatenate([a_ref[g] for g in range(GROUPS)], axis=1)
    summed = h.astype(F32) + jnp.dot(attended, w_out, preferred_element_type=F32)
    center = jnp.mean(summed, axis=1, keepdims=True)
    shifted = summed - center
    spread = jnp.mean(jnp.square(shifted), axis=1, keepdims=True)
    return (shifted * lax.rsqrt(spread + epsilon) * gain_row).astype(BF)


def whole_kernel(
    n, fac_ref, h_ref, marks_ref, dest_ref, w_ref, wo_ref, gain_ref, out_ref,
    k_ref, v_ref, q_ref, a_ref, first_ref, moved_ref, low_ref, high_ref, mlow_ref, mhigh_ref,
    outgoing, arrived, slots_out, slots_in, halo_send, halo_recv, slot_send, slot_recv, row_send, row_recv,
):
    rows, channels = h_ref.shape
    rim = rows // 4
    block = rim
    capacity = outgoing.shape[1]
    me = lax.axis_index("wide")
    right, left = lax.rem(me + 1, n), lax.rem(me + n - 1, n)

    barrier = pltpu.get_barrier_semaphore()

    def greet(t, carry):
        pl.semaphore_signal(
            barrier, inc=1, device_id={"wide": lax.rem(me + t, n)}, device_id_type=pl.DeviceIdType.MESH
        )
        return carry

    lax.fori_loop(1, n, greet, 0)

    def remote(src, dst, send, recv, peer):
        return pltpu.make_async_remote_copy(
            src_ref=src, dst_ref=dst, send_sem=send, recv_sem=recv,
            device_id={"wide": peer}, device_id_type=pl.DeviceIdType.MESH,
        )

    dest = dest_ref[...]
    target = lax.div(dest, jnp.full_like(dest, rows))
    slot = dest - target * rows + 1
    member = lax.broadcasted_iota(jnp.int32, (n, rows), 0) == jnp.broadcast_to(target, (n, rows))
    member = member.astype(F32)
    upper = (
        lax.broadcasted_iota(jnp.int32, (block, block), 0) <= lax.broadcasted_iota(jnp.int32, (block, block), 1)
    ).astype(F32).astype(BF)
    carry = jnp.zeros((n, 1), F32)
    ranks = []
    for r in range(0, rows, block):
        part = member[:, r : r + block]
        ranks.append(jnp.dot(part.astype(BF), upper, preferred_element_type=F32) + carry)
        carry = carry + jnp.sum(part, axis=1, keepdims=True)
    rank = jnp.sum(jnp.concatenate(ranks, axis=1) * member, axis=0, keepdims=True)
    position = rank.astype(jnp.int32) - 1
    width = slots_out.shape[2]
    chosen = (
        lax.broadcasted_iota(jnp.int32, (width, rows), 0) == jnp.broadcast_to(position, (width, rows))
    ).astype(F32).astype(BF)
    coarse = (member * (slot >> 5).astype(F32)).astype(BF)
    fine = (member * (slot & 31).astype(F32)).astype(BF)
    table = lax.dot_general(coarse, chosen, NT, preferred_element_type=F32) * 32.0
    table = (table + lax.dot_general(fine, chosen, NT, preferred_element_type=F32)).astype(jnp.int32)
    for t in range(n):
        slots_out[t] = table[t : t + 1, :]

    for r in range(0, rows, block):
        project_keys(h_ref[r : r + block, :], marks_ref[0:1, r : r + block], w_ref[0], k_ref, v_ref, rim + r)

    pl.semaphore_wait(barrier, n - 1)

    early = (
        (h_ref.at[pl.ds(0, rim)], high_ref.at[0], 0, left),
        (h_ref.at[pl.ds(rows - rim, rim)], low_ref.at[0], 1, right),
        (marks_ref.at[:, pl.ds(0, rim)], mhigh_ref, 2, left),
        (marks_ref.at[:, pl.ds(rows - rim, rim)], mlow_ref, 3, right),
    )
    late = (
        (moved_ref.at[pl.ds(0, rim)], high_ref.at[1], 4, left),
        (moved_ref.at[pl.ds(rows - rim, rim)], low_ref.at[1], 5, right),
    )

    def rim_copy(entry):
        src, dst, number, peer = entry
        return remote(src, dst, halo_send.at[number], halo_recv.at[number], peer)

    for entry in early:
        rim_copy(entry).start()

    def slot_copy(peer, source):
        return remote(slots_out.at[peer], slots_in.at[source], slot_send.at[peer], slot_recv.at[source], peer)

    def send_slots(t, carry):
        slot_copy(lax.rem(me + t, n), me).start()
        return carry

    lax.fori_loop(1, n, send_slots, 0)
    slots_in[me] = slots_out[me]

    def layer_blocks(layer, h_of, store, step, start):
        def one(i, carry):
            r = pl.multiple_of(block * (start + step * i), block)
            store[pl.ds(r, block), :] = attend(
                h_of[pl.ds(r, block), :],
                marks_ref[layer : layer + 1, pl.ds(r, block)],
                layer, fac_ref, w_ref[layer], wo_ref[layer], gain_ref[layer : layer + 1, :],
                k_ref, v_ref, q_ref, a_ref, r, block + 2 * rim,
            )
            return carry

        lax.fori_loop(0, 2, one, 0)

    def layer_rims(layer):
        project_keys(low_ref[layer], mlow_ref[layer : layer + 1, :], w_ref[layer], k_ref, v_ref, 0)
        project_keys(high_ref[layer], mhigh_ref[layer : layer + 1, :], w_ref[layer], k_ref, v_ref, rim + rows)

    layer_blocks(0, h_ref, first_ref, 1, 1)
    for entry in early:
        rim_copy(entry).wait()
    layer_rims(0)
    layer_blocks(0, h_ref, first_ref, 3, 0)

    first = first_ref[...]
    place = lax.broadcasted_iota(jnp.int32, (capacity, rows), 0)

    def gathered(peer):
        wanted = jnp.where(target == peer, position, -1)
        pick = (place == jnp.broadcast_to(wanted, (capacity, rows))).astype(F32).astype(BF)
        return jnp.dot(pick, first, preferred_element_type=F32).astype(BF)

    def peer_at(t):
        odd = lax.rem(t, 2)
        return lax.rem(me + n // 2 + (2 * odd - 1) * ((t + 1) // 2) + n, n)

    def row_copy(peer, source):
        return remote(outgoing.at[peer], arrived.at[source], row_send.at[peer], row_recv.at[source], peer)

    outgoing[peer_at(0)] = gathered(peer_at(0))

    def exchange(t, carry):
        peer = peer_at(t)
        outgoing[peer] = gathered(peer)
        row_copy(peer_at(t - 1), me).start()
        return carry

    lax.fori_loop(1, n - 1, exchange, 0)
    arrived[me] = gathered(me)
    row_copy(peer_at(n - 2), me).start()

    def settle_copies(t, carry):
        other = lax.rem(me + t, n)
        slot_copy(other, other).wait()
        row_copy(other, other).wait()
        return carry

    lax.fori_loop(1, n, settle_copies, 0)

    places = jnp.concatenate([slots_in[t][:, :capacity] for t in range(n)], axis=1)
    came = arrived[...].reshape(n * capacity, channels)

    def land(r):
        here = lax.broadcasted_iota(jnp.int32, (block, n * capacity), 0) + (r + 1)
        pick = (here == jnp.broadcast_to(places, (block, n * capacity))).astype(F32).astype(BF)
        moved_ref[r : r + block, :] = jnp.dot(pick, came, preferred_element_type=F32).astype(BF)

    def own_keys(r):
        project_keys(moved_ref[r : r + block, :], marks_ref[1:2, r : r + block], w_ref[1], k_ref, v_ref, rim + r)

    land(0)
    land(rows - block)
    land(block)
    for entry in late:
        rim_copy(entry).start()
    land(2 * block)
    for r in range(0, rows, block):
        own_keys(r)
    layer_blocks(1, moved_ref, out_ref, 1, 1)
    for entry in late:
        rim_copy(entry).wait()
    layer_rims(1)
    layer_blocks(1, moved_ref, out_ref, 3, 0)


def body(voxels, regular_window, shifted_window, dest, w_qkv, w_out, gain, temper):
    rows, channels = voxels.shape
    n = lax.axis_size("wide")
    rim = rows // 4
    half = channels // GROUPS
    capacity = 2 * rows // n
    factor = temper * (1.0 / math.sqrt(channels // HEADS)) * math.log2(math.e)
    marks = jnp.stack([regular_window, shifted_window]) + 1
    vmem = pl.BlockSpec(memory_space=pltpu.VMEM)
    dma = pltpu.SemaphoreType.DMA
    return pl.pallas_call(
        functools.partial(whole_kernel, n),
        out_shape=jax.ShapeDtypeStruct((rows, channels), BF),
        in_specs=[pl.BlockSpec(memory_space=pltpu.SMEM)] + [vmem] * 6,
        out_specs=vmem,
        scratch_shapes=[
            pltpu.VMEM((GROUPS, half + LANES, rows + 2 * rim), BF),
            pltpu.VMEM((GROUPS, rows + 2 * rim, half), BF),
            pltpu.VMEM((GROUPS, rim, half), BF),
            pltpu.VMEM((GROUPS, rim, half), BF),
            pltpu.VMEM((rows, channels), BF),
            pltpu.VMEM((rows, channels), BF),
            pltpu.VMEM((2, rim, channels), BF),
            pltpu.VMEM((2, rim, channels), BF),
            pltpu.VMEM((2, rim), jnp.int32),
            pltpu.VMEM((2, rim), jnp.int32),
            pltpu.VMEM((n, capacity, channels), BF),
            pltpu.VMEM((n, capacity, channels), BF),
            pltpu.VMEM((n, 1, max(capacity, LANES)), jnp.int32),
            pltpu.VMEM((n, 1, max(capacity, LANES)), jnp.int32),
            dma((6,)), dma((6,)), dma((n,)), dma((n,)), dma((n,)), dma((n,)),
        ],
        compiler_params=pltpu.CompilerParams(
            vmem_limit_bytes=48 << 20, collective_id=0, has_side_effects=True
        ),
    )(factor, voxels, marks, dest[None, :], w_qkv, w_out, gain)


def solution(mesh):
    spread = P(("parts", "wide"))
    wide_rows = P(("parts", "wide"), None)
    return jax.shard_map(
        body,
        mesh=mesh,
        in_specs=(wide_rows, spread, spread, spread, P(), P(), P(), P()),
        out_specs=wide_rows,
        check_vma=False,
    )
```

```python
import functools
import math

import jax
import jax.numpy as jnp
from jax import lax
from jax.experimental import pallas as pl
from jax.experimental.pallas import tpu as pltpu
from jax.sharding import PartitionSpec as P

HEADS = 8
LANES = 128
GROUPS = 2

epsilon = 1e-05
apart = 2.0**100

BF = jnp.bfloat16
F32 = jnp.float32
NT = (((1,), (1,)), ((), ()))


def bit_flags(marks_row):
    count = marks_row.shape[1]
    place = lax.broadcasted_iota(jnp.int32, (LANES, count), 0)
    bit = (jnp.broadcast_to(marks_row, (LANES, count)) >> (place & 31)) & 1
    return jnp.where(place < LANES // 2, bit, 1 - bit).astype(F32)


def project_keys(h, marks_row, w, k_ref, v_ref, first):
    rows, channels = h.shape
    half = channels // GROUPS
    kv = jnp.dot(h, w[:, channels:], preferred_element_type=F32)
    code = ((bit_flags(marks_row) - 1.0) * apart).astype(BF)
    at = pl.ds(first, rows)
    for g in range(GROUPS):
        k_ref[g, :half, at] = jnp.transpose(kv[:, g * half : (g + 1) * half]).astype(BF)
        k_ref[g, half:, at] = code
        v_ref[g, at, :] = kv[:, channels + g * half : channels + (g + 1) * half].astype(BF)


def attend(h, marks_row, layer, fac_ref, w, w_out, gain_row, k_ref, v_ref, first_key, key_rows):
    rows, channels = h.shape
    half = channels // GROUPS
    head_dim = channels // HEADS
    each = HEADS // GROUPS
    q = jnp.dot(h, w[:, :channels], preferred_element_type=F32).astype(BF)
    code = jnp.transpose(bit_flags(marks_row)).astype(BF)
    head_of_lane = lax.broadcasted_iota(jnp.int32, (rows, half), 1) // head_dim
    pairs = [(g, j) for g in range(GROUPS) for j in range(0, each, 2)]

    def scores(pair):
        g, first = pair
        q_half = q[:, g * half : (g + 1) * half]
        stacked = jnp.concatenate(
            [
                jnp.concatenate([jnp.where(head_of_lane == j, q_half, jnp.zeros_like(q_half)), code], axis=1)
                for j in (first, first + 1)
            ],
            axis=0,
        )
        return jnp.dot(stacked, k_ref[g, :, pl.ds(first_key, key_rows)], preferred_element_type=F32)

    outs = [jnp.zeros((rows, half), F32) for _ in range(GROUPS)]
    coming = scores(pairs[0])
    for t, (g, first) in enumerate(pairs):
        both = coming
        if t + 1 < len(pairs):
            coming = scores(pairs[t + 1])
        weights = []
        for i in range(2):
            s = both[i * rows : (i + 1) * rows]
            top = jnp.max(s, axis=1, keepdims=True)
            e = jnp.exp2((s - top) * fac_ref[layer, g * each + first + i])
            weights.append((e * (1.0 / jnp.sum(e, axis=1, keepdims=True))).astype(BF))
        o = jnp.dot(
            jnp.concatenate(weights, axis=0),
            v_ref[g, pl.ds(first_key, key_rows), :],
            preferred_element_type=F32,
        )
        for i in range(2):
            outs[g] = jnp.where(head_of_lane == first + i, o[i * rows : (i + 1) * rows], outs[g])
    attended = jnp.concatenate([o.astype(BF) for o in outs], axis=1)
    summed = h.astype(F32) + jnp.dot(attended, w_out, preferred_element_type=F32)
    center = jnp.mean(summed, axis=1, keepdims=True)
    shifted = summed - center
    spread = jnp.mean(jnp.square(shifted), axis=1, keepdims=True)
    return (shifted * lax.rsqrt(spread + epsilon) * gain_row).astype(BF)


def whole_kernel(
    n, fac_ref, h_ref, marks_ref, dest_ref, w_ref, wo_ref, gain_ref, out_ref,
    k_ref, v_ref, first_ref, moved_ref, low_ref, high_ref, mlow_ref, mhigh_ref,
    outgoing, arrived, slots_out, slots_in, halo_send, halo_recv, slot_send, slot_recv, row_send, row_recv,
):
    rows, channels = h_ref.shape
    rim = rows // 4
    block = rim
    capacity = outgoing.shape[1]
    me = lax.axis_index("wide")
    right, left = lax.rem(me + 1, n), lax.rem(me + n - 1, n)

    barrier = pltpu.get_barrier_semaphore()

    def greet(t, carry):
        pl.semaphore_signal(
            barrier, inc=1, device_id={"wide": lax.rem(me + t, n)}, device_id_type=pl.DeviceIdType.MESH
        )
        return carry

    lax.fori_loop(1, n, greet, 0)

    def remote(src, dst, send, recv, peer):
        return pltpu.make_async_remote_copy(
            src_ref=src, dst_ref=dst, send_sem=send, recv_sem=recv,
            device_id={"wide": peer}, device_id_type=pl.DeviceIdType.MESH,
        )

    dest = dest_ref[...]
    target = lax.div(dest, jnp.full_like(dest, rows))
    slot = dest - target * rows + 1
    member = lax.broadcasted_iota(jnp.int32, (n, rows), 0) == jnp.broadcast_to(target, (n, rows))
    member = member.astype(F32)
    upper = (
        lax.broadcasted_iota(jnp.int32, (block, block), 0) <= lax.broadcasted_iota(jnp.int32, (block, block), 1)
    ).astype(F32).astype(BF)
    carry = jnp.zeros((n, 1), F32)
    ranks = []
    for r in range(0, rows, block):
        part = member[:, r : r + block]
        ranks.append(jnp.dot(part.astype(BF), upper, preferred_element_type=F32) + carry)
        carry = carry + jnp.sum(part, axis=1, keepdims=True)
    rank = jnp.sum(jnp.concatenate(ranks, axis=1) * member, axis=0, keepdims=True)
    position = rank.astype(jnp.int32) - 1
    width = slots_out.shape[2]
    chosen = (
        lax.broadcasted_iota(jnp.int32, (width, rows), 0) == jnp.broadcast_to(position, (width, rows))
    ).astype(F32).astype(BF)
    coarse = (member * (slot >> 5).astype(F32)).astype(BF)
    fine = (member * (slot & 31).astype(F32)).astype(BF)
    table = lax.dot_general(coarse, chosen, NT, preferred_element_type=F32) * 32.0
    table = (table + lax.dot_general(fine, chosen, NT, preferred_element_type=F32)).astype(jnp.int32)
    for t in range(n):
        slots_out[t] = table[t : t + 1, :]

    for r in range(0, rows, block):
        project_keys(h_ref[r : r + block, :], marks_ref[0:1, r : r + block], w_ref[0], k_ref, v_ref, rim + r)

    pl.semaphore_wait(barrier, n - 1)

    early = (
        (h_ref.at[pl.ds(0, rim)], high_ref.at[0], 0, left),
        (h_ref.at[pl.ds(rows - rim, rim)], low_ref.at[0], 1, right),
        (marks_ref.at[:, pl.ds(0, rim)], mhigh_ref, 2, left),
        (marks_ref.at[:, pl.ds(rows - rim, rim)], mlow_ref, 3, right),
    )
    late = (
        (moved_ref.at[pl.ds(0, rim)], high_ref.at[1], 4, left),
        (moved_ref.at[pl.ds(rows - rim, rim)], low_ref.at[1], 5, right),
    )

    def rim_copy(entry):
        src, dst, number, peer = entry
        return remote(src, dst, halo_send.at[number], halo_recv.at[number], peer)

    for entry in early:
        rim_copy(entry).start()

    def slot_copy(peer, source):
        return remote(slots_out.at[peer], slots_in.at[source], slot_send.at[peer], slot_recv.at[source], peer)

    def send_slots(t, carry):
        slot_copy(lax.rem(me + t, n), me).start()
        return carry

    lax.fori_loop(1, n, send_slots, 0)
    slots_in[me] = slots_out[me]

    def layer_blocks(layer, h_of, store, step, start):
        def one(i, carry):
            r = pl.multiple_of(block * (start + step * i), block)
            store[pl.ds(r, block), :] = attend(
                h_of[pl.ds(r, block), :],
                marks_ref[layer : layer + 1, pl.ds(r, block)],
                layer, fac_ref, w_ref[layer], wo_ref[layer], gain_ref[layer : layer + 1, :],
                k_ref, v_ref, r, block + 2 * rim,
            )
            return carry

        lax.fori_loop(0, 2, one, 0)

    def layer_rims(layer):
        project_keys(low_ref[layer], mlow_ref[layer : layer + 1, :], w_ref[layer], k_ref, v_ref, 0)
        project_keys(high_ref[layer], mhigh_ref[layer : layer + 1, :], w_ref[layer], k_ref, v_ref, rim + rows)

    layer_blocks(0, h_ref, first_ref, 1, 1)
    for entry in early:
        rim_copy(entry).wait()
    layer_rims(0)
    layer_blocks(0, h_ref, first_ref, 3, 0)

    first = first_ref[...]
    place = lax.broadcasted_iota(jnp.int32, (capacity, rows), 0)

    def gathered(peer):
        wanted = jnp.where(target == peer, position, -1)
        pick = (place == jnp.broadcast_to(wanted, (capacity, rows))).astype(F32).astype(BF)
        return jnp.dot(pick, first, preferred_element_type=F32).astype(BF)

    def peer_at(t):
        odd = lax.rem(t, 2)
        return lax.rem(me + n // 2 + (2 * odd - 1) * ((t + 1) // 2) + n, n)

    def row_copy(peer, source):
        return remote(outgoing.at[peer], arrived.at[source], row_send.at[peer], row_recv.at[source], peer)

    outgoing[peer_at(0)] = gathered(peer_at(0))

    def exchange(t, carry):
        peer = peer_at(t)
        outgoing[peer] = gathered(peer)
        row_copy(peer_at(t - 1), me).start()
        return carry

    lax.fori_loop(1, n - 1, exchange, 0)
    arrived[me] = gathered(me)
    row_copy(peer_at(n - 2), me).start()

    def settle_copies(t, carry):
        other = lax.rem(me + t, n)
        slot_copy(other, other).wait()
        row_copy(other, other).wait()
        return carry

    lax.fori_loop(1, n, settle_copies, 0)

    places = jnp.concatenate([slots_in[t][:, :capacity] for t in range(n)], axis=1)
    came = arrived[...].reshape(n * capacity, channels)

    def land(r):
        here = lax.broadcasted_iota(jnp.int32, (block, n * capacity), 0) + (r + 1)
        pick = (here == jnp.broadcast_to(places, (block, n * capacity))).astype(F32).astype(BF)
        moved_ref[r : r + block, :] = jnp.dot(pick, came, preferred_element_type=F32).astype(BF)

    def own_keys(r):
        project_keys(moved_ref[r : r + block, :], marks_ref[1:2, r : r + block], w_ref[1], k_ref, v_ref, rim + r)

    land(0)
    land(rows - block)
    land(block)
    for entry in late:
        rim_copy(entry).start()
    land(2 * block)
    for r in range(0, rows, block):
        own_keys(r)
    layer_blocks(1, moved_ref, out_ref, 1, 1)
    for entry in late:
        rim_copy(entry).wait()
    layer_rims(1)
    layer_blocks(1, moved_ref, out_ref, 3, 0)


def body(voxels, regular_window, shifted_window, dest, w_qkv, w_out, gain, temper):
    rows, channels = voxels.shape
    n = lax.axis_size("wide")
    rim = rows // 4
    half = channels // GROUPS
    capacity = 2 * rows // n
    factor = temper * (1.0 / math.sqrt(channels // HEADS)) * math.log2(math.e)
    marks = jnp.stack([regular_window, shifted_window]) + 1
    vmem = pl.BlockSpec(memory_space=pltpu.VMEM)
    dma = pltpu.SemaphoreType.DMA
    return pl.pallas_call(
        functools.partial(whole_kernel, n),
        out_shape=jax.ShapeDtypeStruct((rows, channels), BF),
        in_specs=[pl.BlockSpec(memory_space=pltpu.SMEM)] + [vmem] * 6,
        out_specs=vmem,
        scratch_shapes=[
            pltpu.VMEM((GROUPS, half + LANES, rows + 2 * rim), BF),
            pltpu.VMEM((GROUPS, rows + 2 * rim, half), BF),
            pltpu.VMEM((rows, channels), BF),
            pltpu.VMEM((rows, channels), BF),
            pltpu.VMEM((2, rim, channels), BF),
            pltpu.VMEM((2, rim, channels), BF),
            pltpu.VMEM((2, rim), jnp.int32),
            pltpu.VMEM((2, rim), jnp.int32),
            pltpu.VMEM((n, capacity, channels), BF),
            pltpu.VMEM((n, capacity, channels), BF),
            pltpu.VMEM((n, 1, max(capacity, LANES)), jnp.int32),
            pltpu.VMEM((n, 1, max(capacity, LANES)), jnp.int32),
            dma((6,)), dma((6,)), dma((n,)), dma((n,)), dma((n,)), dma((n,)),
        ],
        compiler_params=pltpu.CompilerParams(
            vmem_limit_bytes=48 << 20, collective_id=0, has_side_effects=True
        ),
    )(factor, voxels, marks, dest[None, :], w_qkv, w_out, gain)


def solution(mesh):
    spread = P(("parts", "wide"))
    wide_rows = P(("parts", "wide"), None)
    return jax.shard_map(
        body,
        mesh=mesh,
        in_specs=(wide_rows, spread, spread, spread, P(), P(), P(), P()),
        out_specs=wide_rows,
        check_vma=False,
    )
```
